256 devices in a mesh: tm: 8 (over x, core), rows: 32 (over y, z).
Axes of the slice: x: 4, y: 4, z: 8, core: 2. Of those that a mesh axis runs over, the one named last changes fastest.
Arguments:
- latent: bfloat16 [32, 192, 128, 128], P('tm', None, 'rows'), may hold values from -6 to 6
- clip_ids: int32 [32], replicated, may hold values from 0 to 3, as said below
- gain_in: float32 [192], replicated, may hold values from 0.1 to 1.9
- conv_in: bfloat16 [3, 3, 3, 96, 192], replicated, may hold values from -0.078125 to 0.078125
- bias_in: float32 [96], replicated, may hold values from -3 to 3
- gain_mid: float32 [96], replicated, may hold values from 0.1 to 1.9
- conv_mid: bfloat16 [3, 3, 3, 96, 96], replicated, may hold values from -0.125 to 0.125
- bias_mid: float32 [96], replicated, may hold values from -3 to 3
- skip_weight: bfloat16 [96, 192], replicated, may hold values from -0.4375 to 0.4375
- skip_bias: float32 [96], replicated, may hold values from -3 to 3
Outputs:
- decoded: bfloat16 [32, 96, 128, 128], P('tm', None, 'rows')
The draws below stay inside these ranges and needn't reach their ends.
Inputs may be any that keep to these rules, and one draw needn't show every extreme that they name: `clip_ids`: clip number of each frame; numbers never fall along the frames and every number appears; each clip lies on consecutive frames, and every clip other than the window's first and last holds 1 + 4 k frames, at most 21.
All inputs are finite; a program needn't handle non-finite values.
Results may differ from the reference program's by a relative error of at most 0.0075.
Values may be sent and summed in bfloat16 or wider, within the bound.
A program may use at most 64 MiB of HBM per device.

```python
import jax
import jax.numpy as jnp
from jax import lax

CIN = 192
COUT = 96
WIDTH = 128
FRAMES = 32
HEIGHT = 128
CLIPS = 4


def draw_clip_ids(key, part):
    inner_count = max(CLIPS - 2, 1)
    step_most = min(5, ((FRAMES - 2) // inner_count - 1) // 4)
    first_key = jax.random.fold_in(key, 11)
    second_key = jax.random.fold_in(key, 23)
    quarter_steps = jax.random.randint(first_key, (CLIPS - 2,), 0, step_most + 1, dtype=jnp.int32)
    lengths = 1 + 4 * quarter_steps
    remain = FRAMES - jnp.sum(lengths)
    opening = jax.random.randint(second_key, (), 1, remain, dtype=jnp.int32)
    bounds = opening + jnp.concatenate([jnp.zeros((1,), jnp.int32), jnp.cumsum(lengths).astype(jnp.int32)])
    frames = jnp.arange(FRAMES, dtype=jnp.int32)
    return jnp.sum((frames[:, None] >= bounds[None, :]).astype(jnp.int32), axis=1).astype(jnp.int32)


def shard_levels(key, extent, split, low, top_value):
    def one(axis_at, parts):
        draws = jax.random.uniform(jax.random.fold_in(jax.random.fold_in(key, 6), axis_at), (parts,), jnp.float32, low / len(split), top_value / len(split))
        return jnp.repeat(jnp.exp(draws), extent[axis_at] // parts).reshape((-1,) + (1,) * (len(extent) - axis_at - 1))

    level = one(*split[0])
    for cut in split[1:]:
        level = level * one(*cut)
    return level


def centred(key, dims, spread, limit, split=(), kind=jnp.bfloat16):
    array = spread * jax.random.normal(key, dims, jnp.float32)
    if split:
        array = array * shard_levels(key, dims, split, -0.22, 0.18)
    return jnp.clip(array, -limit, limit).astype(kind)


def setup_inputs(seed: int = 0) -> dict:
    seeds = jax.random.split(jax.random.key(seed), 11)
    latent = centred(seeds[0], (FRAMES, CIN, HEIGHT, WIDTH), 1.0, 6.0, ((0, 8), (2, 32)))
    clip_ids = draw_clip_ids(jax.random.fold_in(seeds[10], 71), 0)
    gain_in = jnp.clip(1.0 + 0.18 * jax.random.normal(seeds[2], (CIN,), jnp.float32), 0.1, 1.9)
    conv_in = centred(seeds[3], (3, 3, 3, COUT, CIN), (27 * CIN) ** -0.5, 0.078125)
    bias_in = centred(seeds[4], (COUT,), 0.5, 3.0, (), jnp.float32)
    gain_mid = jnp.clip(1.0 + 0.18 * jax.random.normal(seeds[5], (COUT,), jnp.float32), 0.1, 1.9)
    conv_mid = centred(seeds[6], (3, 3, 3, COUT, COUT), (27 * COUT) ** -0.5, 0.125)
    bias_mid = centred(seeds[7], (COUT,), 0.5, 3.0, (), jnp.float32)
    skip_weight = centred(seeds[8], (COUT, CIN), CIN ** -0.5, 0.4375)
    skip_bias = centred(seeds[9], (COUT,), 0.5, 3.0, (), jnp.float32)
    return {"latent": latent, "clip_ids": clip_ids, "gain_in": gain_in, "conv_in": conv_in, "bias_in": bias_in, "gain_mid": gain_mid, "conv_mid": conv_mid, "bias_mid": bias_mid, "skip_weight": skip_weight, "skip_bias": skip_bias}


def keep_table(clip_ids, start, count):
    frames = start + jnp.arange(count, dtype=jnp.int32)
    final_index = clip_ids.shape[0] - 1
    own_clip = jnp.take(clip_ids, jnp.clip(frames, 0, final_index))
    tables = []
    for back_step in range(3):
        source = frames - back_step
        src_clip = jnp.take(clip_ids, jnp.clip(source, 0, final_index))
        tables.append(((source >= 0) & (src_clip == own_clip)).astype(jnp.float32))
    return jnp.stack(tables)

def norm_silu(values, gain):
    floats = values.astype(jnp.float32)
    mean_sq = lax.optimization_barrier(jnp.mean(floats * floats, axis=1, keepdims=True))
    scaled = floats * lax.rsqrt(mean_sq + 1e-06) * gain[None, :, None, None]
    return jax.nn.silu(scaled).astype(jnp.bfloat16)

def causal_conv(padded, weight, keep, out_frames, out_rows):
    wide = jnp.pad(padded, ((0, 0), (0, 0), (0, 0), (1, 1)))
    width_all = padded.shape[3]
    total = jnp.zeros((out_frames, weight.shape[3], out_rows, width_all), jnp.float32)
    for t_tap in range(3):
        part = jnp.zeros_like(total)
        for h_tap in range(3):
            for w_tap in range(3):
                slab = wide[t_tap:t_tap + out_frames, :, h_tap:h_tap + out_rows, w_tap:w_tap + width_all]
                part = part + jnp.einsum('oc,fcrw->forw', weight[t_tap, h_tap, w_tap].astype(jnp.float32), slab.astype(jnp.float32))
        total = total + part * keep[2 - t_tap][:, None, None, None]
    return total

def reference(latent, clip_ids, gain_in, conv_in, bias_in, gain_mid, conv_mid, bias_mid, skip_weight, skip_bias):
    frames_all = latent.shape[0]
    height_all = latent.shape[2]
    keep = keep_table(clip_ids, 0, frames_all)
    first = norm_silu(latent, gain_in)
    first_pad = jnp.pad(first, ((2, 0), (0, 0), (1, 1), (0, 0)))

    def layer_one(index):
        window = lax.dynamic_slice_in_dim(first_pad, index, 3, 0)
        mask = lax.dynamic_slice_in_dim(keep, index, 1, 1)
        result = causal_conv(window, conv_in, mask, 1, height_all)[0]
        return (result + bias_in[:, None, None]).astype(jnp.bfloat16)
    hidden = lax.map(layer_one, jnp.arange(frames_all, dtype=jnp.int32))
    second = norm_silu(hidden, gain_mid)
    second_pad = jnp.pad(second, ((2, 0), (0, 0), (1, 1), (0, 0)))

    def layer_two(index):
        window = lax.dynamic_slice_in_dim(second_pad, index, 3, 0)
        mask = lax.dynamic_slice_in_dim(keep, index, 1, 1)
        tail = causal_conv(window, conv_mid, mask, 1, height_all)[0]
        frame = lax.dynamic_index_in_dim(latent, index, 0, keepdims=False)
        short = jnp.einsum('oc,crw->orw', skip_weight.astype(jnp.float32), frame.astype(jnp.float32))
        return (tail + bias_mid[:, None, None] + short + skip_bias[:, None, None]).astype(jnp.bfloat16)
    return lax.map(layer_two, jnp.arange(frames_all, dtype=jnp.int32))
```

```python
import jax
import jax.numpy as jnp
from jax import lax
from jax.experimental import pallas as pl
from jax.experimental.pallas import tpu as pltpu
from jax.sharding import PartitionSpec as P

MESH = pl.DeviceIdType.MESH
F32 = jnp.float32
BF16 = jnp.bfloat16
EPS = 1e-6
LANES = 128
PARTS = ((1, 2), (0, 3))


def column(row_ref, scale=1.0):
    size = row_ref.shape[1]
    down = lax.broadcasted_iota(jnp.int32, (size, size), 0)
    across = lax.broadcasted_iota(jnp.int32, (size, size), 1)
    picked = jnp.where(down == across, row_ref[...] * scale, 0.0)
    return jnp.broadcast_to(jnp.sum(picked, axis=1, keepdims=True), (size, LANES))


def norm_silu(values, half_gain):
    mean_sq = jnp.mean(values * values, axis=0, keepdims=True)
    half = values * lax.rsqrt(mean_sq + EPS) * half_gain
    return half + half * jnp.tanh(half)


def put_shifts(x_ref, frame, row, values):
    lane = lax.broadcasted_iota(jnp.int32, values.shape, 1)
    left = jnp.where(lane == 0, 0.0, pltpu.roll(values, 1, 1))
    right = jnp.where(lane == LANES - 1, 0.0, pltpu.roll(values, LANES - 1, 1))
    x_ref[frame, row, 0] = left.astype(BF16)
    x_ref[frame, row, 2] = right.astype(BF16)


def body(
    n_t,
    n_r,
    latent_hbm,
    clips,
    gain_in,
    conv_in_hbm,
    bias_in,
    gain_mid,
    conv_mid_hbm,
    bias_mid,
    skip_hbm,
    skip_bias,
    out_hbm,
    latent_v,
    wide,
    raw,
    x1,
    x2,
    taps1,
    taps2,
    w1,
    w2,
    w_skip,
    col_in,
    col_bias,
    col_mid,
    col_out,
    acc1,
    acc2,
    sent1,
    got1,
    sent2,
    got2,
    packed,
    out_v,
    load_sem,
    store_sem,
    row_send,
    row_recv,
    time_send,
    time_recv,
):
    t_at = lax.axis_index("tm")
    r_at = lax.axis_index("rows")
    up, down = lax.rem(r_at + n_r - 1, n_r), lax.rem(r_at + 1, n_r)
    before, after = lax.rem(t_at + n_t - 1, n_t), lax.rem(t_at + 1, n_t)

    loads = {}
    for k, frame in enumerate((2, 3, 0, 1)):
        loads[frame] = pltpu.make_async_copy(latent_hbm.at[frame], latent_v.at[frame], load_sem.at[k])
    for k, (src, dst) in enumerate(((conv_in_hbm, taps1), (conv_mid_hbm, taps2), (skip_hbm, w_skip))):
        loads["w%d" % k] = pltpu.make_async_copy(src, dst, load_sem.at[4 + k])
    for copy in loads.values():
        copy.start()

    barrier = pltpu.get_barrier_semaphore()
    for peer in ({"rows": up}, {"rows": down}, {"tm": before}, {"tm": after}):
        pl.semaphore_signal(barrier, inc=1, device_id=peer, device_id_type=MESH)

    total = clips.shape[0]

    def keep(frame, back):
        at = t_at * 4 + frame
        own = clips[jnp.minimum(at, total - 1)]
        past = clips[jnp.clip(at - back, 0, total - 1)]
        good = (own == past) & (at < total) & (at >= back)
        return jnp.where(good, 1.0, 0.0).astype(F32)

    keeps = {(f, d): keep(f, d) for f in range(1, 6) for d in (1, 2) if 0 <= f - d < 4}
    live = {0: jnp.where(r_at > 0, 1.0, 0.0).astype(F32), 5: jnp.where(r_at < n_r - 1, 1.0, 0.0).astype(F32)}

    col_in[...] = column(gain_in, 0.5)
    col_bias[...] = column(bias_in)
    col_mid[...] = column(gain_mid, 0.5)
    col_out[...] = column(bias_mid) + column(skip_bias)

    def row_copies(x_ref, first, slot):
        pair = pl.ds(first, 2)
        return [
            pltpu.make_async_remote_copy(
                src_ref=x_ref.at[pair, mine, 1],
                dst_ref=x_ref.at[pair, theirs, 1],
                send_sem=row_send.at[slot + k],
                recv_sem=row_recv.at[slot + k],
                device_id={"rows": peer},
                device_id_type=MESH,
            )
            for k, (mine, theirs, peer) in enumerate(((1, 5, up), (4, 0, down)))
        ]

    def time_copy(src, dst, part, slot):
        return pltpu.make_async_remote_copy(
            src_ref=src.at[part],
            dst_ref=dst.at[part],
            send_sem=time_send.at[slot],
            recv_sem=time_recv.at[slot],
            device_id={"tm": after},
            device_id_type=MESH,
        )

    rows1 = {2: row_copies(x1, 2, 0), 0: row_copies(x1, 0, 2)}
    rows2 = {2: row_copies(x2, 2, 4), 0: row_copies(x2, 0, 6)}
    times1 = [time_copy(sent1, got1, part, part) for part in range(2)]
    times2 = [time_copy(sent2, got2, part, 2 + part) for part in range(2)]

    def start(copies):
        for copy in copies:
            copy.start()

    def first_act(frame, rows):
        for row in rows:
            values = wide[frame, pl.ds(row, 192, stride=4), :]
            raw[frame, row] = values.astype(BF16)
            act = norm_silu(values, col_in[...])
            x1[frame, row + 1, 1] = act.astype(BF16)
            put_shifts(x1, frame, row + 1, act)

    def halo(x_ref, copies, first):
        for row, copy in ((5, copies[0]), (0, copies[1])):
            copy.wait_recv()
            for frame in (first, first + 1):
                values = x_ref[frame, row, 1].astype(F32) * live[row]
                x_ref[frame, row, 1] = values.astype(BF16)
                put_shifts(x_ref, frame, row, values)

    seen = {}

    def conv(weight, x_ref, acc, first, rows, base):
        spots = [(f, r) for r in rows for f in (first, first + 1)]
        depth = 9 * x_ref.shape[3]
        slab = jnp.concatenate([x_ref[f, pl.ds(r, 3)].reshape(depth, LANES) for f, r in spots], axis=1)
        terms = jnp.dot(weight[...], slab, preferred_element_type=F32)
        sums = {}
        for k, (f, r) in enumerate(spots):
            for tap in range(3):
                value = terms[tap * 96 : (tap + 1) * 96, k * LANES : (k + 1) * LANES]
                target = f + 2 - tap
                if target > f:
                    value = value * keeps[target, target - f]
                key = (target, r)
                sums[key] = value if key not in sums else sums[key] + value
        for (target, r), value in sums.items():
            key = (id(acc), target, r)
            if key in seen:
                value = value + acc[target, r]
            elif target < 4 and base is not None:
                value = value + base
            seen[key] = True
            acc[target, r] = value

    def pass_on(acc, buf, copies, part):
        for g in range(2):
            for k, row in enumerate(PARTS[part]):
                buf[part, g, k] = acc[4 + g, row].astype(BF16)
        copies[part].start()

    def second_act(frame, part):
        for k, row in enumerate(PARTS[part]):
            values = acc1[frame, row]
            if frame < 2:
                values = values + got1[part, frame, k].astype(F32)
            act = norm_silu(values, col_mid[...])
            x2[frame, row + 1, 1] = act.astype(BF16)
            put_shifts(x2, frame, row + 1, act)

    def shortcut(rows):
        spots = [(f, r) for r in rows for f in range(4)]
        slab = jnp.concatenate([raw[f, r] for f, r in spots], axis=1)
        terms = jnp.dot(w_skip[...], slab, preferred_element_type=F32)
        for k, (f, r) in enumerate(spots):
            acc2[f, r] = terms[:, k * LANES : (k + 1) * LANES] + col_out[...]
            seen[id(acc2), f, r] = True

    def finish(frame):
        for part in range(2):
            for k, row in enumerate(PARTS[part]):
                values = acc2[frame, row]
                if frame < 2:
                    values = values + got2[part, frame, k].astype(F32)
                packed[frame, pl.ds(row, 96, stride=4), :] = values
        out_v[frame] = packed[frame].astype(BF16)
        copy = pltpu.make_async_copy(out_v.at[frame], out_hbm.at[frame], store_sem.at[frame])
        copy.start()
        return copy

    for frame in (2, 3):
        loads[frame].wait()
        wide[frame] = latent_v[frame].astype(F32)
        first_act(frame, (0, 3))
    pl.semaphore_wait(barrier, 4)
    start(rows1[2])
    for frame in (0, 1):
        loads[frame].wait()
        wide[frame] = latent_v[frame].astype(F32)
        first_act(frame, (0, 3))
    start(rows1[0])
    for k in range(3):
        loads["w%d" % k].wait()
    for tap in range(3):
        w1[pl.ds(tap * 96, 96), :] = jnp.concatenate([taps1[tap * 9 + k] for k in range(9)], axis=1)
        w2[pl.ds(tap * 96, 96), :] = jnp.concatenate([taps2[tap * 9 + k] for k in range(9)], axis=1)
    for frame in (2, 3, 0, 1):
        first_act(frame, (1, 2))

    conv(w1, x1, acc1, 2, (1, 2), col_bias[...])
    pass_on(acc1, sent1, times1, 0)
    conv(w1, x1, acc1, 0, (1, 2), col_bias[...])
    for row in range(4):
        shortcut((row,))
    halo(x1, rows1[2], 2)
    conv(w1, x1, acc1, 2, (0, 3), col_bias[...])
    pass_on(acc1, sent1, times1, 1)
    halo(x1, rows1[0], 0)
    conv(w1, x1, acc1, 0, (0, 3), col_bias[...])

    for frame in (2, 3):
        second_act(frame, 1)
    start(rows2[2])
    for frame in (2, 3):
        second_act(frame, 0)
    conv(w2, x2, acc2, 2, (1, 2), None)
    pass_on(acc2, sent2, times2, 0)
    times1[1].wait_recv()
    for frame in (0, 1):
        second_act(frame, 1)
    start(rows2[0])
    times1[0].wait_recv()
    for frame in (0, 1):
        second_act(frame, 0)
    conv(w2, x2, acc2, 0, (1, 2), None)
    halo(x2, rows2[2], 2)
    conv(w2, x2, acc2, 2, (0, 3), None)
    pass_on(acc2, sent2, times2, 1)
    halo(x2, rows2[0], 0)
    conv(w2, x2, acc2, 0, (0, 3), None)
    stores = [finish(2), finish(3)]
    times2[0].wait_recv()
    times2[1].wait_recv()
    stores += [finish(0), finish(1)]
    for copy in stores:
        copy.wait()
    for copy in rows1[2] + rows1[0] + rows2[2] + rows2[0] + times1 + times2:
        copy.wait_send()


def block(n_t, n_r, latent, clips, gain_in, conv_in, bias_in, gain_mid, conv_mid, bias_mid, skip_weight, skip_bias):
    hbm = pl.BlockSpec(memory_space=pl.ANY)
    vmem = pl.BlockSpec(memory_space=pltpu.VMEM)
    smem = pl.BlockSpec(memory_space=pltpu.SMEM)
    dma = pltpu.SemaphoreType.DMA
    out = pl.pallas_call(
        lambda *refs: body(n_t, n_r, *refs),
        out_shape=jax.ShapeDtypeStruct((4, 384, LANES), BF16),
        in_specs=[hbm, smem, vmem, hbm, vmem, vmem, hbm, vmem, hbm, vmem],
        out_specs=hbm,
        scratch_shapes=[
            pltpu.VMEM((4, 768, LANES), BF16),
            pltpu.VMEM((4, 768, LANES), F32),
            pltpu.VMEM((4, 4, 192, LANES), BF16),
            pltpu.VMEM((4, 6, 3, 192, LANES), BF16),
            pltpu.VMEM((4, 6, 3, 96, LANES), BF16),
            pltpu.VMEM((27, 96, 192), BF16),
            pltpu.VMEM((27, 96, 96), BF16),
            pltpu.VMEM((288, 1728), BF16),
            pltpu.VMEM((288, 864), BF16),
            pltpu.VMEM((96, 192), BF16),
            pltpu.VMEM((192, LANES), F32),
            pltpu.VMEM((96, LANES), F32),
            pltpu.VMEM((96, LANES), F32),
            pltpu.VMEM((96, LANES), F32),
            pltpu.VMEM((6, 4, 96, LANES), F32),
            pltpu.VMEM((6, 4, 96, LANES), F32),
            pltpu.VMEM((2, 2, 2, 96, LANES), BF16),
            pltpu.VMEM((2, 2, 2, 96, LANES), BF16),
            pltpu.VMEM((2, 2, 2, 96, LANES), BF16),
            pltpu.VMEM((2, 2, 2, 96, LANES), BF16),
            pltpu.VMEM((4, 384, LANES), F32),
            pltpu.VMEM((4, 384, LANES), BF16),
            dma((7,)),
            dma((4,)),
            dma((8,)),
            dma((8,)),
            dma((4,)),
            dma((4,)),
        ],
        compiler_params=pltpu.CompilerParams(
            collective_id=0, has_side_effects=True, vmem_limit_bytes=40 * 1024 * 1024
        ),
        name="residual_block",
    )(
        latent.reshape(4, 768, LANES),
        clips,
        gain_in.reshape(1, 192),
        conv_in.reshape(27, 96, 192),
        bias_in.reshape(1, 96),
        gain_mid.reshape(1, 96),
        conv_mid.reshape(27, 96, 96),
        bias_mid.reshape(1, 96),
        skip_weight,
        skip_bias.reshape(1, 96),
    )
    return out.reshape(4, 96, 4, LANES)


def solution(mesh):
    n_t, n_r = mesh.shape["tm"], mesh.shape["rows"]
    return jax.shard_map(
        lambda *args: block(n_t, n_r, *args),
        mesh=mesh,
        in_specs=(P("tm", None, "rows", None),) + (P(),) * 9,
        out_specs=P("tm", None, "rows", None),
        check_vma=False,
    )
```

```python
import jax
import jax.numpy as jnp
from jax import lax
from jax.experimental import pallas as pl
from jax.experimental.pallas import tpu as pltpu
from jax.sharding import PartitionSpec as P

MESH = pl.DeviceIdType.MESH
F32 = jnp.float32
BF16 = jnp.bfloat16
EPS = 1e-6
LANES = 128
PARTS = ((1, 2), (0, 3))


def column(row_ref, scale=1.0):
    size = row_ref.shape[1]
    down = lax.broadcasted_iota(jnp.int32, (size, size), 0)
    across = lax.broadcasted_iota(jnp.int32, (size, size), 1)
    picked = jnp.where(down == across, row_ref[...] * scale, 0.0)
    return jnp.broadcast_to(jnp.sum(picked, axis=1, keepdims=True), (size, LANES))


def norm_silu(values, half_gain):
    mean_sq = jnp.mean(values * values, axis=0, keepdims=True)
    half = values * lax.rsqrt(mean_sq + EPS) * half_gain
    return half + half * jnp.tanh(half)


def put_shifts(x_ref, frame, row, values):
    lane = lax.broadcasted_iota(jnp.int32, values.shape, 1)
    left = jnp.where(lane == 0, 0.0, pltpu.roll(values, 1, 1))
    right = jnp.where(lane == LANES - 1, 0.0, pltpu.roll(values, LANES - 1, 1))
    x_ref[frame, row, 0] = left.astype(BF16)
    x_ref[frame, row, 2] = right.astype(BF16)


def body(
    n_t,
    n_r,
    latent_hbm,
    clips_hbm,
    gain_in_hbm,
    conv_in_hbm,
    bias_in_hbm,
    gain_mid_hbm,
    conv_mid_hbm,
    bias_mid_hbm,
    skip_hbm,
    skip_bias_hbm,
    out_hbm,
    clips,
    gain_in,
    bias_in,
    gain_mid,
    bias_mid,
    skip_bias,
    latent_v,
    wide,
    raw,
    x1,
    x2,
    taps1,
    taps2,
    w1,
    w2,
    w_skip,
    col_in,
    col_bias,
    col_mid,
    col_out,
    acc1,
    acc2,
    sent1,
    got1,
    sent2,
    got2,
    packed,
    out_v,
    load_sem,
    store_sem,
    row_send,
    row_recv,
    time_send,
    time_recv,
):
    t_at = lax.axis_index("tm")
    r_at = lax.axis_index("rows")
    up, down = lax.rem(r_at + n_r - 1, n_r), lax.rem(r_at + 1, n_r)
    before, after = lax.rem(t_at + n_t - 1, n_t), lax.rem(t_at + 1, n_t)

    loads = {}
    for k, frame in enumerate((2, 3, 0, 1)):
        loads[frame] = pltpu.make_async_copy(latent_hbm.at[frame], latent_v.at[frame], load_sem.at[k])
    for k, (src, dst) in enumerate(((conv_in_hbm, taps1), (conv_mid_hbm, taps2), (skip_hbm, w_skip))):
        loads["w%d" % k] = pltpu.make_async_copy(src, dst, load_sem.at[4 + k])
    small = (
        (clips_hbm, clips),
        (gain_in_hbm, gain_in),
        (bias_in_hbm, bias_in),
        (gain_mid_hbm, gain_mid),
        (bias_mid_hbm, bias_mid),
        (skip_bias_hbm, skip_bias),
    )
    small = [pltpu.make_async_copy(src, dst, load_sem.at[7 + k]) for k, (src, dst) in enumerate(small)]
    for copy in small + list(loads.values()):
        copy.start()

    barrier = pltpu.get_barrier_semaphore()
    for peer in ({"rows": up}, {"rows": down}, {"tm": before}, {"tm": after}):
        pl.semaphore_signal(barrier, inc=1, device_id=peer, device_id_type=MESH)

    for copy in small:
        copy.wait()
    total = clips.shape[0]

    def keep(frame, back):
        at = t_at * 4 + frame
        own = clips[jnp.minimum(at, total - 1)]
        past = clips[jnp.clip(at - back, 0, total - 1)]
        good = (own == past) & (at < total) & (at >= back)
        return jnp.where(good, 1.0, 0.0).astype(F32)

    keeps = {(f, d): keep(f, d) for f in range(1, 6) for d in (1, 2) if 0 <= f - d < 4}
    live = {0: jnp.where(r_at > 0, 1.0, 0.0).astype(F32), 5: jnp.where(r_at < n_r - 1, 1.0, 0.0).astype(F32)}

    col_in[...] = column(gain_in, 0.5)
    col_bias[...] = column(bias_in)
    col_mid[...] = column(gain_mid, 0.5)
    col_out[...] = column(bias_mid) + column(skip_bias)

    def row_copies(x_ref, first, slot):
        pair = pl.ds(first, 2)
        return [
            pltpu.make_async_remote_copy(
                src_ref=x_ref.at[pair, mine, 1],
                dst_ref=x_ref.at[pair, theirs, 1],
                send_sem=row_send.at[slot + k],
                recv_sem=row_recv.at[slot + k],
                device_id={"rows": peer},
                device_id_type=MESH,
            )
            for k, (mine, theirs, peer) in enumerate(((1, 5, up), (4, 0, down)))
        ]

    def time_copy(src, dst, part, slot):
        return pltpu.make_async_remote_copy(
            src_ref=src.at[part],
            dst_ref=dst.at[part],
            send_sem=time_send.at[slot],
            recv_sem=time_recv.at[slot],
            device_id={"tm": after},
            device_id_type=MESH,
        )

    rows1 = {2: row_copies(x1, 2, 0), 0: row_copies(x1, 0, 2)}
    rows2 = {2: row_copies(x2, 2, 4), 0: row_copies(x2, 0, 6)}
    times1 = [time_copy(sent1, got1, part, part) for part in range(2)]
    times2 = [time_copy(sent2, got2, part, 2 + part) for part in range(2)]

    def start(copies):
        for copy in copies:
            copy.start()

    def first_act(frame, rows):
        for row in rows:
            values = wide[frame, pl.ds(row, 192, stride=4), :]
            raw[frame, row] = values.astype(BF16)
            act = norm_silu(values, col_in[...])
            x1[frame, row + 1, 1] = act.astype(BF16)
            put_shifts(x1, frame, row + 1, act)

    def halo(x_ref, copies, first):
        for row, copy in ((5, copies[0]), (0, copies[1])):
            copy.wait_recv()
            for frame in (first, first + 1):
                values = x_ref[frame, row, 1].astype(F32) * live[row]
                x_ref[frame, row, 1] = values.astype(BF16)
                put_shifts(x_ref, frame, row, values)

    seen = {}

    def conv(weight, x_ref, acc, first, rows, base):
        spots = [(f, r) for r in rows for f in (first, first + 1)]
        depth = 9 * x_ref.shape[3]
        slab = jnp.concatenate([x_ref[f, pl.ds(r, 3)].reshape(depth, LANES) for f, r in spots], axis=1)
        terms = jnp.dot(weight[...], slab, preferred_element_type=F32)
        sums = {}
        for k, (f, r) in enumerate(spots):
            for tap in range(3):
                value = terms[tap * 96 : (tap + 1) * 96, k * LANES : (k + 1) * LANES]
                target = f + 2 - tap
                if target > f:
                    value = value * keeps[target, target - f]
                key = (target, r)
                sums[key] = value if key not in sums else sums[key] + value
        for (target, r), value in sums.items():
            key = (id(acc), target, r)
            if key in seen:
                value = value + acc[target, r]
            elif target < 4 and base is not None:
                value = value + base
            seen[key] = True
            acc[target, r] = value

    def pass_on(acc, buf, copies, part):
        for g in range(2):
            for k, row in enumerate(PARTS[part]):
                buf[part, g, k] = acc[4 + g, row].astype(BF16)
        copies[part].start()

    def second_act(frame, part):
        for k, row in enumerate(PARTS[part]):
            values = acc1[frame, row]
            if frame < 2:
                values = values + got1[part, frame, k].astype(F32)
            act = norm_silu(values, col_mid[...])
            x2[frame, row + 1, 1] = act.astype(BF16)
            put_shifts(x2, frame, row + 1, act)

    def shortcut(rows):
        spots = [(f, r) for r in rows for f in range(4)]
        slab = jnp.concatenate([raw[f, r] for f, r in spots], axis=1)
        terms = jnp.dot(w_skip[...], slab, preferred_element_type=F32)
        for k, (f, r) in enumerate(spots):
            acc2[f, r] = terms[:, k * LANES : (k + 1) * LANES] + col_out[...]
            seen[id(acc2), f, r] = True

    def finish(frame):
        for part in range(2):
            for k, row in enumerate(PARTS[part]):
                values = acc2[frame, row]
                if frame < 2:
                    values = values + got2[part, frame, k].astype(F32)
                packed[frame, pl.ds(row, 96, stride=4), :] = values
        out_v[frame] = packed[frame].astype(BF16)
        copy = pltpu.make_async_copy(out_v.at[frame], out_hbm.at[frame], store_sem.at[frame])
        copy.start()
        return copy

    for frame in (2, 3):
        loads[frame].wait()
        wide[frame] = latent_v[frame].astype(F32)
        first_act(frame, (0, 3))
    pl.semaphore_wait(barrier, 4)
    start(rows1[2])
    for frame in (0, 1):
        loads[frame].wait()
        wide[frame] = latent_v[frame].astype(F32)
        first_act(frame, (0, 3))
    start(rows1[0])
    for k in range(3):
        loads["w%d" % k].wait()
    for tap in range(3):
        w1[pl.ds(tap * 96, 96), :] = jnp.concatenate([taps1[tap * 9 + k] for k in range(9)], axis=1)
        w2[pl.ds(tap * 96, 96), :] = jnp.concatenate([taps2[tap * 9 + k] for k in range(9)], axis=1)
    for frame in (2, 3, 0, 1):
        first_act(frame, (1, 2))

    conv(w1, x1, acc1, 2, (1, 2), col_bias[...])
    pass_on(acc1, sent1, times1, 0)
    conv(w1, x1, acc1, 0, (1, 2), col_bias[...])
    for row in range(4):
        shortcut((row,))
    halo(x1, rows1[2], 2)
    conv(w1, x1, acc1, 2, (0, 3), col_bias[...])
    pass_on(acc1, sent1, times1, 1)
    halo(x1, rows1[0], 0)
    conv(w1, x1, acc1, 0, (0, 3), col_bias[...])

    for frame in (2, 3):
        second_act(frame, 1)
    start(rows2[2])
    for frame in (2, 3):
        second_act(frame, 0)
    conv(w2, x2, acc2, 2, (1, 2), None)
    pass_on(acc2, sent2, times2, 0)
    times1[1].wait_recv()
    for frame in (0, 1):
        second_act(frame, 1)
    start(rows2[0])
    times1[0].wait_recv()
    for frame in (0, 1):
        second_act(frame, 0)
    conv(w2, x2, acc2, 0, (1, 2), None)
    halo(x2, rows2[2], 2)
    conv(w2, x2, acc2, 2, (0, 3), None)
    pass_on(acc2, sent2, times2, 1)
    halo(x2, rows2[0], 0)
    conv(w2, x2, acc2, 0, (0, 3), None)
    stores = [finish(2), finish(3)]
    times2[0].wait_recv()
    times2[1].wait_recv()
    stores += [finish(0), finish(1)]
    for copy in stores:
        copy.wait()
    for copy in rows1[2] + rows1[0] + rows2[2] + rows2[0] + times1 + times2:
        copy.wait_send()


def block(n_t, n_r, latent, clips, gain_in, conv_in, bias_in, gain_mid, conv_mid, bias_mid, skip_weight, skip_bias):
    hbm = pl.BlockSpec(memory_space=pltpu.HBM)
    dma = pltpu.SemaphoreType.DMA
    out = pl.pallas_call(
        lambda *refs: body(n_t, n_r, *refs),
        out_shape=jax.ShapeDtypeStruct((4, 384, LANES), BF16),
        in_specs=[hbm] * 10,
        out_specs=pl.BlockSpec(memory_space=pl.ANY),
        scratch_shapes=[
            pltpu.SMEM(clips.shape, jnp.int32),
            pltpu.VMEM((1, 192), F32),
            pltpu.VMEM((1, 96), F32),
            pltpu.VMEM((1, 96), F32),
            pltpu.VMEM((1, 96), F32),
            pltpu.VMEM((1, 96), F32),
            pltpu.VMEM((4, 768, LANES), BF16),
            pltpu.VMEM((4, 768, LANES), F32),
            pltpu.VMEM((4, 4, 192, LANES), BF16),
            pltpu.VMEM((4, 6, 3, 192, LANES), BF16),
            pltpu.VMEM((4, 6, 3, 96, LANES), BF16),
            pltpu.VMEM((27, 96, 192), BF16),
            pltpu.VMEM((27, 96, 96), BF16),
            pltpu.VMEM((288, 1728), BF16),
            pltpu.VMEM((288, 864), BF16),
            pltpu.VMEM((96, 192), BF16),
            pltpu.VMEM((192, LANES), F32),
            pltpu.VMEM((96, LANES), F32),
            pltpu.VMEM((96, LANES), F32),
            pltpu.VMEM((96, LANES), F32),
            pltpu.VMEM((6, 4, 96, LANES), F32),
            pltpu.VMEM((6, 4, 96, LANES), F32),
            pltpu.VMEM((2, 2, 2, 96, LANES), BF16),
            pltpu.VMEM((2, 2, 2, 96, LANES), BF16),
            pltpu.VMEM((2, 2, 2, 96, LANES), BF16),
            pltpu.VMEM((2, 2, 2, 96, LANES), BF16),
            pltpu.VMEM((4, 384, LANES), F32),
            pltpu.VMEM((4, 384, LANES), BF16),
            dma((13,)),
            dma((4,)),
            dma((8,)),
            dma((8,)),
            dma((4,)),
            dma((4,)),
        ],
        compiler_params=pltpu.CompilerParams(
            collective_id=0, has_side_effects=True, vmem_limit_bytes=64 * 1024 * 1024
        ),
        name="residual_block",
    )(
        latent.reshape(4, 768, LANES),
        clips,
        gain_in.reshape(1, 192),
        conv_in.reshape(27, 96, 192),
        bias_in.reshape(1, 96),
        gain_mid.reshape(1, 96),
        conv_mid.reshape(27, 96, 96),
        bias_mid.reshape(1, 96),
        skip_weight,
        skip_bias.reshape(1, 96),
    )
    return out.reshape(4, 96, 4, LANES)


def solution(mesh):
    n_t, n_r = mesh.shape["tm"], mesh.shape["rows"]
    return jax.shard_map(
        lambda *args: block(n_t, n_r, *args),
        mesh=mesh,
        in_specs=(P("tm", None, "rows", None),) + (P(),) * 9,
        out_specs=P("tm", None, "rows", None),
        check_vma=False,
    )
```

```python
import jax
import jax.numpy as jnp
from jax import lax
from jax.experimental import pallas as pl
from jax.experimental.pallas import tpu as pltpu
from jax.sharding import PartitionSpec as P

MESH = pl.DeviceIdType.MESH
F32 = jnp.float32
BF16 = jnp.bfloat16
EPS = 1e-6
LANES = 128
PARTS = ((1, 2), (0, 3))


def column(row_ref, scale=1.0):
    size = row_ref.shape[1]
    down = lax.broadcasted_iota(jnp.int32, (size, size), 0)
    across = lax.broadcasted_iota(jnp.int32, (size, size), 1)
    picked = jnp.where(down == across, row_ref[...] * scale, 0.0)
    return jnp.broadcast_to(jnp.sum(picked, axis=1, keepdims=True), (size, LANES))


def norm_silu(values, half_gain):
    mean_sq = jnp.mean(values * values, axis=0, keepdims=True)
    half = values * lax.rsqrt(mean_sq + EPS) * half_gain
    return half + half * jnp.tanh(half)


def put_shifts(x_ref, frame, row, values):
    lane = lax.broadcasted_iota(jnp.int32, values.shape, 1)
    left = jnp.where(lane == 0, 0.0, pltpu.roll(values, 1, 1))
    right = jnp.where(lane == LANES - 1, 0.0, pltpu.roll(values, LANES - 1, 1))
    x_ref[frame, row, 0] = left.astype(BF16)
    x_ref[frame, row, 2] = right.astype(BF16)


class Exchange:
    def __init__(self, copies, sends, receives):
        self.copies, self.sends, self.receives = copies, sends, receives

    def start(self):
        @pl.when(self.sends)
        def _():
            for copy in self.copies:
                copy.start()

    def wait_recv(self):
        @pl.when(self.receives)
        def _():
            for copy in self.copies:
                copy.wait_recv()

    def wait_send(self):
        @pl.when(self.sends)
        def _():
            for copy in self.copies:
                copy.wait_send()


def body(
    n_t,
    n_r,
    latent_hbm,
    clips_hbm,
    gain_in_hbm,
    conv_in_hbm,
    bias_in_hbm,
    gain_mid_hbm,
    conv_mid_hbm,
    bias_mid_hbm,
    skip_hbm,
    skip_bias_hbm,
    out_ref,
    clips,
    gain_in,
    bias_in,
    gain_mid,
    bias_mid,
    skip_bias,
    latent_v,
    wide,
    raw,
    x1,
    x2,
    taps1,
    taps2,
    w1,
    w1_low,
    w2,
    w_skip,
    col_in,
    col_bias,
    col_mid,
    col_out,
    acc1,
    acc2,
    edge_out,
    edge_in,
    sent1,
    got1,
    sent2,
    got2,
    packed,
    load_sem,
    row_send,
    row_recv,
    time_send,
    time_recv,
):
    t_at = lax.axis_index("tm")
    r_at = lax.axis_index("rows")
    has_up, has_down = r_at > 0, r_at < n_r - 1
    has_before, has_after = t_at > 0, t_at < n_t - 1
    up, down, before, after = {"rows": r_at - 1}, {"rows": r_at + 1}, {"tm": t_at - 1}, {"tm": t_at + 1}

    barrier = pltpu.get_barrier_semaphore()
    for there, peer in ((has_up, up), (has_down, down), (has_before, before)):

        @pl.when(there)
        def _(peer=peer):
            pl.semaphore_signal(barrier, inc=1, device_id=peer, device_id_type=MESH)

    pairs = [(latent_hbm.at[f], latent_v.at[f]) for f in (2, 3, 0, 1)]
    pairs += [(conv_in_hbm, taps1), (gain_in_hbm, gain_in), (clips_hbm, clips), (bias_in_hbm, bias_in)]
    pairs += [(gain_mid_hbm, gain_mid), (bias_mid_hbm, bias_mid), (skip_bias_hbm, skip_bias)]
    pairs += [(skip_hbm, w_skip), (conv_mid_hbm, taps2)]
    order = [0, 1, 5, 4, 2, 3, 6, 7, 8, 9, 10, 11, 12]
    loads = [pltpu.make_async_copy(src, dst, load_sem.at[k]) for k, (src, dst) in enumerate(pairs)]
    for k in order:
        loads[k].start()
    latent_load = {2: loads[0], 3: loads[1], 0: loads[2], 1: loads[3]}

    @pl.when(jnp.logical_not(has_up))
    def _():
        edge_in[1] = jnp.zeros(edge_in.shape[1:], BF16)
        x2[:, 0] = jnp.zeros((4, 3, 96, LANES), BF16)

    @pl.when(jnp.logical_not(has_down))
    def _():
        edge_in[0] = jnp.zeros(edge_in.shape[1:], BF16)
        x2[:, 5] = jnp.zeros((4, 3, 96, LANES), BF16)

    @pl.when(jnp.logical_not(has_before))
    def _():
        got1[...] = jnp.zeros(got1.shape, BF16)
        got2[...] = jnp.zeros(got2.shape, BF16)

    def remote(src, dst, send_sem, recv_sem, peer):
        return pltpu.make_async_remote_copy(
            src_ref=src, dst_ref=dst, send_sem=send_sem, recv_sem=recv_sem, device_id=peer, device_id_type=MESH
        )

    def by_row(src_of, dst_of, slot):
        return [
            Exchange([remote(src_of(k), dst_of(k), row_send.at[slot + k], row_recv.at[slot + k], peer)], sends, gets)
            for k, (peer, sends, gets) in enumerate(((up, has_up, has_down), (down, has_down, has_up)))
        ]

    def by_time(src, dst, part, slot):
        copy = remote(src.at[part], dst.at[part], time_send.at[slot], time_recv.at[slot], after)
        return Exchange([copy], has_after, has_before)

    rows1 = {g: by_row(lambda k: edge_out.at[k, pl.ds(g, 2)], lambda k: edge_in.at[k, pl.ds(g, 2)], g) for g in (4, 2, 0)}
    rows2 = {
        f: by_row(lambda k: x2.at[pl.ds(f, 2), (1, 4)[k], 1], lambda k: x2.at[pl.ds(f, 2), (5, 0)[k], 1], 6 + f)
        for f in (2, 0)
    }
    times1 = [by_time(sent1, got1, part, part) for part in range(2)]
    times2 = [by_time(sent2, got2, part, 2 + part) for part in range(2)]

    def start(copies):
        for copy in copies:
            copy.start()

    def arrived(copies):
        for copy in copies:
            copy.wait_recv()

    def spread(frame):
        latent_load[frame].wait()
        wide[frame] = latent_v[frame].astype(F32)

    def first_act(frame, rows):
        for row in rows:
            values = wide[frame, pl.ds(row, 192, stride=4), :]
            raw[frame, row] = values.astype(BF16)
            act = norm_silu(values, col_in[...])
            x1[frame, row, 1] = act.astype(BF16)
            put_shifts(x1, frame, row, act)

    seen = set()

    def gather(acc, spots, terms, base):
        sums = {}
        for k, (f, r) in enumerate(spots):
            for tap in range(3):
                value = terms[tap * 96 : (tap + 1) * 96, k * LANES : (k + 1) * LANES]
                target = f + 2 - tap
                if target > f:
                    value = value * keeps[target, target - f]
                key = (target, r)
                sums[key] = value if key not in sums else sums[key] + value
        for (target, r), value in sums.items():
            key = (id(acc), target, r)
            if key in seen:
                value = value + acc[target, r]
            elif target < 4 and base is not None and 1 <= r <= 4:
                value = value + base
            seen.add(key)
            acc[target, r] = value

    def conv1(first, targets):
        taps = {-1: (0,), 0: (1, 0), 1: (0, 1, 2), 2: (1, 2, 3), 3: (2, 3), 4: (3,)}
        for target in targets:
            rows = taps[target]
            frames = (first, first + 1)
            slab = jnp.concatenate(
                [
                    jnp.concatenate([x1[f, row].reshape(576, LANES) for row in rows], axis=0)
                    for f in frames
                ],
                axis=1,
            )
            weight = w1_low if target < 1 else w1
            terms = jnp.dot(weight[:, : 576 * len(rows)], slab, preferred_element_type=F32)
            gather(acc1, [(f, target + 1) for f in frames], terms, col_bias[...])

    def conv2(first, rows):
        spots = [(f, r) for r in rows for f in (first, first + 1)]
        slab = jnp.concatenate([x2[f, pl.ds(r, 3)].reshape(864, LANES) for f, r in spots], axis=1)
        gather(acc2, spots, jnp.dot(w2[...], slab, preferred_element_type=F32), None)

    def edges_out(g):
        for k, row in enumerate((0, 5)):
            for frame in (g, g + 1):
                edge_out[k, frame] = acc1[frame, row].astype(BF16)
        start(rows1[g])

    def pass_on(value, buf, copies, part):
        for g in range(2):
            for k, row in enumerate(PARTS[part]):
                buf[part, g, k] = value(4 + g, row).astype(BF16)
        copies[part].start()

    def hidden(frame, row):
        values = acc1[frame, row + 1]
        if row in (0, 3):
            values = values + edge_in[1 if row == 0 else 0, frame].astype(F32)
        return values

    def second_act(frame, part):
        for k, row in enumerate(PARTS[part]):
            values = hidden(frame, row)
            if frame < 2:
                values = values + got1[part, frame, k].astype(F32)
            act = norm_silu(values, col_mid[...])
            x2[frame, row + 1, 1] = act.astype(BF16)
            put_shifts(x2, frame, row + 1, act)

    def halo2(first):
        arrived(rows2[first])
        for row in (0, 5):
            for frame in (first, first + 1):
                put_shifts(x2, frame, row, x2[frame, row, 1].astype(F32))

    def shortcut(row):
        slab = jnp.concatenate([raw[f, row] for f in range(4)], axis=1)
        terms = jnp.dot(w_skip[...], slab, preferred_element_type=F32)
        for f in range(4):
            acc2[f, row] = terms[:, f * LANES : (f + 1) * LANES] + col_out[...]
            seen.add((id(acc2), f, row))

    def finish(frame):
        for part in range(2):
            for k, row in enumerate(PARTS[part]):
                values = acc2[frame, row]
                if frame < 2:
                    values = values + got2[part, frame, k].astype(F32)
                packed[frame, pl.ds(row, 96, stride=4), :] = values
        out_ref[frame] = packed[frame].astype(BF16)

    loads[5].wait()
    col_in[...] = column(gain_in, 0.5)
    for frame in (2, 3):
        spread(frame)
        first_act(frame, (0, 3))
    loads[4].wait()
    for tap in range(3):
        at = pl.ds(tap * 96, 96)
        w1[at, :] = jnp.concatenate([taps1[tap * 9 + k] for k in range(9)], axis=1)
        w1_low[at, :] = jnp.concatenate([taps1[tap * 9 + k] for k in (6, 7, 8, 3, 4, 5)], axis=1)
    for k in (6, 7, 8, 9, 10):
        loads[k].wait()
    total = clips.shape[0]

    def keep(frame, back):
        at = t_at * 4 + frame
        own = clips[jnp.minimum(at, total - 1)]
        past = clips[jnp.clip(at - back, 0, total - 1)]
        good = (own == past) & (at < total) & (at >= back)
        return jnp.where(good, 1.0, 0.0).astype(F32)

    keeps = {(f, d): keep(f, d) for f in range(1, 6) for d in (1, 2) if 0 <= f - d < 4}
    col_bias[...] = column(bias_in)
    col_mid[...] = column(gain_mid, 0.5)
    col_out[...] = column(bias_mid) + column(skip_bias)

    conv1(2, (-1, 4))
    friends = has_up.astype(jnp.int32) + has_down.astype(jnp.int32) + has_after.astype(jnp.int32)
    pl.semaphore_wait(barrier, friends)
    edges_out(4)
    for frame in (0, 1):
        spread(frame)
        first_act(frame, (0, 3))
    conv1(0, (-1, 4))
    edges_out(2)
    edges_out(0)
    for frame in (2, 3):
        first_act(frame, (1, 2))
    conv1(2, (1, 2))
    pass_on(lambda g, row: acc1[g, row + 1], sent1, times1, 0)
    conv1(2, (0, 3))
    arrived(rows1[4])
    pass_on(hidden, sent1, times1, 1)
    for frame in (0, 1):
        first_act(frame, (1, 2))
    conv1(0, (0, 3, 1, 2))
    loads[12].wait()
    for tap in range(3):
        w2[pl.ds(tap * 96, 96), :] = jnp.concatenate([taps2[tap * 9 + k] for k in range(9)], axis=1)
    arrived(rows1[2])
    for frame in (2, 3):
        second_act(frame, 1)
    start(rows2[2])
    for frame in (2, 3):
        second_act(frame, 0)
    loads[11].wait()
    for row in range(4):
        shortcut(row)
    conv2(2, (1, 2))
    pass_on(lambda g, row: acc2[g, row], sent2, times2, 0)
    arrived(rows1[0])
    arrived(times1)
    for frame in (0, 1):
        second_act(frame, 1)
    start(rows2[0])
    for frame in (0, 1):
        second_act(frame, 0)
    conv2(0, (1, 2))
    halo2(2)
    conv2(2, (0, 3))
    pass_on(lambda g, row: acc2[g, row], sent2, times2, 1)
    halo2(0)
    conv2(0, (0, 3))
    finish(2)
    finish(3)
    arrived(times2)
    finish(0)
    finish(1)
    for copy in rows1[4] + rows1[2] + rows1[0] + rows2[2] + rows2[0] + times1 + times2:
        copy.wait_send()


def block(n_t, n_r, latent, clips, gain_in, conv_in, bias_in, gain_mid, conv_mid, bias_mid, skip_weight, skip_bias):
    hbm = pl.BlockSpec(memory_space=pltpu.HBM)
    dma = pltpu.SemaphoreType.DMA
    out = pl.pallas_call(
        lambda *refs: body(n_t, n_r, *refs),
        out_shape=pltpu.VMEM((4, 384, LANES), BF16),
        in_specs=[hbm] * 10,
        out_specs=pl.BlockSpec(memory_space=pltpu.VMEM),
        scratch_shapes=[
            pltpu.SMEM(clips.shape, jnp.int32),
            pltpu.VMEM((1, 192), F32),
            pltpu.VMEM((1, 96), F32),
            pltpu.VMEM((1, 96), F32),
            pltpu.VMEM((1, 96), F32),
            pltpu.VMEM((1, 96), F32),
            pltpu.VMEM((4, 768, LANES), BF16),
            pltpu.VMEM((4, 768, LANES), F32),
            pltpu.VMEM((4, 4, 192, LANES), BF16),
            pltpu.VMEM((4, 4, 3, 192, LANES), BF16),
            pltpu.VMEM((4, 6, 3, 96, LANES), BF16),
            pltpu.VMEM((27, 96, 192), BF16),
            pltpu.VMEM((27, 96, 96), BF16),
            pltpu.VMEM((288, 1728), BF16),
            pltpu.VMEM((288, 1152), BF16),
            pltpu.VMEM((288, 864), BF16),
            pltpu.VMEM((96, 192), BF16),
            pltpu.VMEM((192, LANES), F32),
            pltpu.VMEM((96, LANES), F32),
            pltpu.VMEM((96, LANES), F32),
            pltpu.VMEM((96, LANES), F32),
            pltpu.VMEM((6, 6, 96, LANES), F32),
            pltpu.VMEM((6, 4, 96, LANES), F32),
            pltpu.VMEM((2, 6, 96, LANES), BF16),
            pltpu.VMEM((2, 6, 96, LANES), BF16),
            pltpu.VMEM((2, 2, 2, 96, LANES), BF16),
            pltpu.VMEM((2, 2, 2, 96, LANES), BF16),
            pltpu.VMEM((2, 2, 2, 96, LANES), BF16),
            pltpu.VMEM((2, 2, 2, 96, LANES), BF16),
            pltpu.VMEM((4, 384, LANES), F32),
            dma((13,)),
            dma((10,)),
            dma((10,)),
            dma((4,)),
            dma((4,)),
        ],
        compiler_params=pltpu.CompilerParams(
            collective_id=0, has_side_effects=True, vmem_limit_bytes=48 * 1024 * 1024
        ),
        name="residual_block",
    )(
        *(
            pltpu.with_memory_space_constraint(operand, pltpu.HBM)
            for operand in (
                latent.reshape(4, 768, LANES),
                clips,
                gain_in.reshape(1, 192),
                conv_in.reshape(27, 96, 192),
                bias_in.reshape(1, 96),
                gain_mid.reshape(1, 96),
                conv_mid.reshape(27, 96, 96),
                bias_mid.reshape(1, 96),
                skip_weight,
                skip_bias.reshape(1, 96),
            )
        )
    )
    return out.reshape(4, 96, 4, LANES)


def solution(mesh):
    n_t, n_r = mesh.shape["tm"], mesh.shape["rows"]
    return jax.shard_map(
        lambda *args: block(n_t, n_r, *args),
        mesh=mesh,
        in_specs=(P("tm", None, "rows", None),) + (P(),) * 9,
        out_specs=P("tm", None, "rows", None),
        check_vma=False,
    )
```

```python
import jax
import jax.numpy as jnp
from jax import lax
from jax.experimental import pallas as pl
from jax.experimental.pallas import tpu as pltpu
from jax.sharding import PartitionSpec as P

MESH = pl.DeviceIdType.MESH
F32 = jnp.float32
BF16 = jnp.bfloat16
EPS = 1e-6
LANES = 128
PARTS = ((1, 2), (0, 3))


def column(row_ref, scale=1.0):
    size = row_ref.shape[1]
    down = lax.broadcasted_iota(jnp.int32, (size, size), 0)
    across = lax.broadcasted_iota(jnp.int32, (size, size), 1)
    picked = jnp.where(down == across, row_ref[...] * scale, 0.0)
    return jnp.broadcast_to(jnp.sum(picked, axis=1, keepdims=True), (size, LANES))


def norm_silu(values, half_gain):
    mean_sq = jnp.mean(values * values, axis=0, keepdims=True)
    half = values * lax.rsqrt(mean_sq + EPS) * half_gain
    return half + half * jnp.tanh(half)


def put_shifts(x_ref, frame, row, values):
    lane = lax.broadcasted_iota(jnp.int32, values.shape, 1)
    left = jnp.where(lane == 0, 0.0, pltpu.roll(values, 1, 1))
    right = jnp.where(lane == LANES - 1, 0.0, pltpu.roll(values, LANES - 1, 1))
    x_ref[frame, row, 0] = left.astype(BF16)
    x_ref[frame, row, 2] = right.astype(BF16)


class Exchange:
    def __init__(self, copy, sends, gets):
        self.copy, self.sends, self.gets = copy, sends, gets


def body(
    n_t,
    n_r,
    latent_hbm,
    clips_hbm,
    gain_in_hbm,
    conv_in_hbm,
    bias_in_hbm,
    gain_mid_hbm,
    conv_mid_hbm,
    bias_mid_hbm,
    skip_hbm,
    skip_bias_hbm,
    out_ref,
    clips,
    gain_in,
    bias_in,
    gain_mid,
    bias_mid,
    skip_bias,
    latent_v,
    wide,
    raw,
    x1,
    x2,
    taps1,
    taps2,
    w1,
    w1_low,
    w2,
    w2_low,
    w_skip,
    col_in,
    col_bias,
    col_mid,
    col_out,
    acc1,
    acc2,
    edge_out,
    edge_in,
    corner_out1,
    corner_in1,
    corner_out2,
    corner_in2,
    sent1,
    got1,
    sent2,
    got2,
    packed,
    load_sem,
    row_send,
    row_recv,
    time_send,
    time_recv,
):
    t_at = lax.axis_index("tm")
    r_at = lax.axis_index("rows")
    has_up, has_down = r_at > 0, r_at < n_r - 1
    up, down = {"rows": r_at - 1}, {"rows": r_at + 1}
    before, after = {"tm": lax.rem(t_at + n_t - 1, n_t)}, {"tm": lax.rem(t_at + 1, n_t)}

    barrier = pltpu.get_barrier_semaphore()
    def greet(*peers):
        for peer in peers:
            pl.semaphore_signal(barrier, inc=1, device_id=peer, device_id_type=MESH)

    greet(before)
    pl.when(has_up)(lambda: greet(up, before | up))
    pl.when(has_down)(lambda: greet(down, before | down))

    def load(src, dst, slot):
        return pltpu.make_async_copy(src, dst, load_sem.at[slot])

    load_gain = load(gain_in_hbm, gain_in, 0)
    load_latent = {f: load(latent_hbm.at[f], latent_v.at[f], 1 + f) for f in (2, 3, 0, 1)}
    load_taps = {i: load(conv_in_hbm.at[:, i], taps1.at[:, i], 5 + i) for i in (0, 2, 1)}
    load_clips = load(clips_hbm, clips, 8)
    load_bias = load(bias_in_hbm, bias_in, 9)
    load_mid = [load(gain_mid_hbm, gain_mid, 10), load(bias_mid_hbm, bias_mid, 11), load(skip_bias_hbm, skip_bias, 12)]
    load_mid += [load(skip_hbm, w_skip, 13), load(conv_mid_hbm, taps2, 14)]
    first_loads = [load_gain, load_clips, load_latent[2], load_latent[3], load_taps[0], load_taps[2]]
    first_loads += [load_latent[0], load_latent[1]]
    late_loads = [load_taps[1], load_bias] + load_mid
    for copy in first_loads + late_loads:
        copy.start()

    def clear(ref, *at):
        part = ref.at[at] if at else ref
        part[...] = jnp.zeros(part.shape, BF16)

    @pl.when(jnp.logical_not(has_up))
    def _():
        clear(edge_in, 1)
        clear(corner_in1, 1)
        clear(corner_in2, 1)
        for f in range(4):
            clear(x2, f, 0)

    @pl.when(jnp.logical_not(has_down))
    def _():
        clear(edge_in, 0)
        clear(corner_in1, 0)
        clear(corner_in2, 0)
        for f in range(4):
            clear(x2, f, 5)

    def remote(src, dst, sems, slot, peer, sends=None, gets=None):
        copy = pltpu.make_async_remote_copy(
            src_ref=src,
            dst_ref=dst,
            send_sem=sems[0].at[slot],
            recv_sem=sems[1].at[slot],
            device_id=peer,
            device_id_type=MESH,
        )
        return copy if sends is None else Exchange(copy, sends, gets)

    row_sems, time_sems = (row_send, row_recv), (time_send, time_recv)
    sides = ((up, has_up, has_down), (down, has_down, has_up))

    def by_row(src_of, dst_of, slot):
        return [remote(src_of(k), dst_of(k), row_sems, slot + k, *side) for k, side in enumerate(sides)]

    def by_corner(src, dst, slot):
        return [
            remote(src.at[k], dst.at[k], row_sems, slot + k, after | peer, sends, gets)
            for k, (peer, sends, gets) in enumerate(sides)
        ]

    def by_time(src, dst, slot):
        return [
            remote(src.at[part], dst.at[part], time_sems, slot + part, after) for part in range(2)
        ]

    rows1 = {g: by_row(lambda k: edge_out.at[k, pl.ds(g, 2)], lambda k: edge_in.at[k, pl.ds(g, 2)], g) for g in (2, 0)}
    rows2 = {
        f: by_row(lambda k: x2.at[pl.ds(f, 2), (1, 4)[k], 1], lambda k: x2.at[pl.ds(f, 2), (5, 0)[k], 1], 4 + f)
        for f in (2, 0)
    }
    corners1 = by_corner(corner_out1, corner_in1, 8)
    corners2 = by_corner(corner_out2, corner_in2, 10)
    times1 = by_time(sent1, got1, 0)
    times2 = by_time(sent2, got2, 2)

    def start(*exchanges):
        for sides_of in zip(*exchanges):

            @pl.when(sides_of[0].sends)
            def _(sides_of=sides_of):
                for exchange in sides_of:
                    exchange.copy.start()

    def arrived(*exchanges):
        for sides_of in zip(*exchanges):

            @pl.when(sides_of[0].gets)
            def _(sides_of=sides_of):
                for exchange in sides_of:
                    exchange.copy.wait_recv()

    def left(*exchanges):
        for sides_of in zip(*exchanges):

            @pl.when(sides_of[0].sends)
            def _(sides_of=sides_of):
                for exchange in sides_of:
                    exchange.copy.wait_send()

    def spread(frame):
        wide[frame] = latent_v[frame].astype(F32)

    def first_act(frame, rows):
        for row in rows:
            values = wide[frame, pl.ds(row, 192, stride=4), :]
            raw[frame, row] = values.astype(BF16)
            act = norm_silu(values, col_in[...])
            x1[frame, row, 1] = act.astype(BF16)
            put_shifts(x1, frame, row, act)

    seen = set()

    def gather(acc, first, row, terms, taps, base, keeps_target):
        sums = {}
        for k, f in enumerate((first, first + 1)):
            for n, tap in enumerate(taps):
                target = f + 2 - tap
                if not keeps_target(target):
                    continue
                value = terms[n * 96 : (n + 1) * 96, k * LANES : (k + 1) * LANES]
                if target > f:
                    value = value * keeps[target, target - f]
                sums[target] = value if target not in sums else sums[target] + value
        for target, value in sums.items():
            key = (id(acc), target, row)
            if key in seen:
                value = value + acc[target, row]
            elif base is not None and target < 4 and 1 <= row <= 4:
                value = value + base
            seen.add(key)
            acc[target, row] = value

    sources = {-1: (0,), 0: (1, 0), 1: (0, 1, 2), 2: (1, 2, 3), 3: (2, 3), 4: (3,)}

    def conv1(first, targets):
        for target in targets:
            rows = sources[target]
            slab = jnp.concatenate(
                [jnp.concatenate([x1[f, row].reshape(576, LANES) for row in rows], axis=0) for f in (first, first + 1)],
                axis=1,
            )
            weight = (w1_low if target < 1 else w1)[:, : 576 * len(rows)]
            terms = jnp.dot(weight, slab, preferred_element_type=F32)
            gather(acc1, first, target + 1, terms, (0, 1, 2), col_bias[...] if 0 <= target < 4 else None, lambda g: True)

    def conv2_part(first, target, rows, weight, taps, keeps_target):
        slab = jnp.concatenate(
            [jnp.concatenate([x2[f, row + 1].reshape(288, LANES) for row in rows], axis=0) for f in (first, first + 1)],
            axis=1,
        )
        weight = weight[pl.ds(96 * taps[0], 96 * len(taps)), : 288 * len(rows)]
        terms = jnp.dot(weight, slab, preferred_element_type=F32)
        gather(acc2, first, target + 1, terms, taps, None, keeps_target)

    def conv2(first, targets):
        for target in targets:
            weight = w2_low if target < 1 else w2
            if target in (-1, 4):
                conv2_part(first, target, sources[target], weight, (0, 1), lambda g: g >= 4)
            else:
                conv2_part(first, target, sources[target], weight, (0, 1, 2), lambda g: True)

    def halo2(first):
        for row in (0, 5):
            for frame in (first, first + 1):
                put_shifts(x2, frame, row, x2[frame, row, 1].astype(F32))
        taps = (1, 2) if first == 2 else (0, 1, 2)
        conv2_part(first, 0, (-1,), w2, taps, lambda g: g < 4)
        conv2_part(first, 3, (4,), w2_low, taps, lambda g: g < 4)

    def edges_out(g):
        for k, row in enumerate((0, 5)):
            for frame in (g, g + 1):
                edge_out[k, frame] = acc1[frame, row].astype(BF16)

    def corners_out(acc, buf):
        for k, row in enumerate((0, 5)):
            for g in range(2):
                buf[k, g] = acc[4 + g, row].astype(BF16)

    def pass_on(acc, buf, copies, part):
        for g in range(2):
            for k, row in enumerate(PARTS[part]):
                buf[part, g, k] = acc[4 + g, row + 1].astype(BF16)
        copies[part].start()

    def with_time(values, frame, row, got, corner):
        if frame < 2:
            part = 1 if row in (0, 3) else 0
            values = values + got[part, frame, PARTS[part].index(row)].astype(F32)
            if part:
                values = values + corner[1 if row == 0 else 0, frame].astype(F32)
        return values

    def second_act(frame, part, shifted=True):
        for row in PARTS[part]:
            values = acc1[frame, row + 1]
            if part:
                values = values + edge_in[1 if row == 0 else 0, frame].astype(F32)
            values = with_time(values, frame, row, got1, corner_in1)
            act = norm_silu(values, col_mid[...])
            x2[frame, row + 1, 1] = act.astype(BF16)
            if shifted:
                put_shifts(x2, frame, row + 1, act)

    def shift_edges(first):
        for frame in (first, first + 1):
            for row in (1, 4):
                put_shifts(x2, frame, row, x2[frame, row, 1].astype(F32))

    def shortcut(row):
        slab = jnp.concatenate([raw[f, row] for f in range(4)], axis=1)
        terms = jnp.dot(w_skip[...], slab, preferred_element_type=F32)
        for f in range(4):
            acc2[f, row + 1] = terms[:, f * LANES : (f + 1) * LANES] + col_out[...]
            seen.add((id(acc2), f, row + 1))

    def finish(frame, part):
        for row in PARTS[part]:
            packed[frame, pl.ds(row, 96, stride=4), :] = with_time(acc2[frame, row + 1], frame, row, got2, corner_in2)

    def pack(dst, src, block, row_tap, size):
        for tap in range(3):
            dst[pl.ds(tap * 96, 96), pl.ds(block * 3 * size, 3 * size)] = jnp.concatenate(
                [src[tap, row_tap, k] for k in range(3)], axis=1
            )

    load_gain.wait()
    col_in[...] = column(gain_in, 0.5)
    load_clips.wait()
    total = clips.shape[0]

    def keep(frame, back):
        at = t_at * 4 + frame
        own = clips[jnp.minimum(at, total - 1)]
        past = clips[jnp.clip(at - back, 0, total - 1)]
        good = (own == past) & (at < total) & (at >= back)
        return jnp.where(good, 1.0, 0.0).astype(F32)

    keeps = {(f, d): keep(f, d) for f in range(1, 6) for d in (1, 2) if 0 <= f - d < 4}
    for copy in first_loads[2:]:
        copy.wait()
    pack(w1, taps1, 0, 0, 192)
    pack(w1_low, taps1, 0, 2, 192)
    for frame in (2, 3, 0, 1):
        spread(frame)
        first_act(frame, (0, 3))
    conv1(2, (-1, 4))
    conv1(0, (-1, 4))
    edges_out(2)
    edges_out(0)
    corners_out(acc1, corner_out1)
    greeted = 1 + 2 * has_up.astype(jnp.int32) + 2 * has_down.astype(jnp.int32)
    pl.semaphore_wait(barrier, greeted)
    start(rows1[2], corners1, rows1[0])
    load_taps[1].wait()
    load_bias.wait()
    col_bias[...] = column(bias_in)
    for tap in range(3):
        rest = [taps1[tap, i, k] for i in (0, 1, 2) for k in range(3)]
        w1[pl.ds(tap * 96, 96), :] = jnp.concatenate(rest, axis=1)
        w1_low[pl.ds(tap * 96, 96), :] = jnp.concatenate(rest[6:] + rest[3:6], axis=1)
    for frame in (2, 3):
        first_act(frame, (1, 2))
    conv1(2, (0, 3))
    pass_on(acc1, sent1, times1, 1)
    conv1(2, (1, 2))
    pass_on(acc1, sent1, times1, 0)
    for frame in (0, 1):
        first_act(frame, (1, 2))
    conv1(0, (0, 3, 1, 2))
    for copy in load_mid:
        copy.wait()
    col_mid[...] = column(gain_mid, 0.5)
    col_out[...] = column(bias_mid) + column(skip_bias)
    for tap in range(3):
        rest = [taps2[tap, i, k] for i in (0, 1, 2) for k in range(3)]
        w2[pl.ds(tap * 96, 96), :] = jnp.concatenate(rest, axis=1)
        w2_low[pl.ds(tap * 96, 96), :] = jnp.concatenate(rest[6:] + rest[3:6], axis=1)
    for frame in (2, 3):
        second_act(frame, 0)
    for row in range(4):
        shortcut(row)
    arrived(rows1[2])
    for frame in (2, 3):
        second_act(frame, 1, shifted=False)
    start(rows2[2])
    shift_edges(2)
    conv2(2, (-1, 4))
    corners_out(acc2, corner_out2)
    start(corners2)
    conv2(2, (0, 3))
    pass_on(acc2, sent2, times2, 1)
    arrived(rows1[0], corners1)
    times1[1].wait_recv()
    for frame in (0, 1):
        second_act(frame, 1, shifted=False)
    start(rows2[0])
    shift_edges(0)
    conv2(2, (1, 2))
    pass_on(acc2, sent2, times2, 0)
    times1[0].wait_recv()
    for frame in (0, 1):
        second_act(frame, 0)
    conv2(0, (0, 3, 1, 2))
    arrived(rows2[2])
    halo2(2)
    for frame in (2, 3):
        finish(frame, 0)
    times2[0].wait_recv()
    times2[1].wait_recv()
    arrived(corners2, rows2[0])
    for frame in (0, 1):
        finish(frame, 0)
    halo2(0)
    for frame in range(4):
        finish(frame, 1)
        out_ref[frame] = packed[frame].astype(BF16)
    left(rows1[2], rows1[0], rows2[2], rows2[0], corners1, corners2)
    for copy in times1 + times2:
        copy.wait_send()


def block(n_t, n_r, latent, clips, gain_in, conv_in, bias_in, gain_mid, conv_mid, bias_mid, skip_weight, skip_bias):
    hbm = pl.BlockSpec(memory_space=pltpu.HBM)
    dma = pltpu.SemaphoreType.DMA
    out = pl.pallas_call(
        lambda *refs: body(n_t, n_r, *refs),
        out_shape=pltpu.VMEM((4, 384, LANES), BF16),
        in_specs=[hbm] * 10,
        out_specs=pl.BlockSpec(memory_space=pltpu.VMEM),
        scratch_shapes=[
            pltpu.SMEM(clips.shape, jnp.int32),
            pltpu.VMEM((1, 192), F32),
            pltpu.VMEM((1, 96), F32),
            pltpu.VMEM((1, 96), F32),
            pltpu.VMEM((1, 96), F32),
            pltpu.VMEM((1, 96), F32),
            pltpu.VMEM((4, 768, LANES), BF16),
            pltpu.VMEM((4, 768, LANES), F32),
            pltpu.VMEM((4, 4, 192, LANES), BF16),
            pltpu.VMEM((4, 4, 3, 192, LANES), BF16),
            pltpu.VMEM((4, 6, 3, 96, LANES), BF16),
            pltpu.VMEM((3, 3, 3, 96, 192), BF16),
            pltpu.VMEM((3, 3, 3, 96, 96), BF16),
            pltpu.VMEM((288, 1728), BF16),
            pltpu.VMEM((288, 1152), BF16),
            pltpu.VMEM((288, 864), BF16),
            pltpu.VMEM((288, 576), BF16),
            pltpu.VMEM((96, 192), BF16),
            pltpu.VMEM((192, LANES), F32),
            pltpu.VMEM((96, LANES), F32),
            pltpu.VMEM((96, LANES), F32),
            pltpu.VMEM((96, LANES), F32),
            pltpu.VMEM((6, 6, 96, LANES), F32),
            pltpu.VMEM((6, 6, 96, LANES), F32),
            pltpu.VMEM((2, 4, 96, LANES), BF16),
            pltpu.VMEM((2, 4, 96, LANES), BF16),
            pltpu.VMEM((2, 2, 96, LANES), BF16),
            pltpu.VMEM((2, 2, 96, LANES), BF16),
            pltpu.VMEM((2, 2, 96, LANES), BF16),
            pltpu.VMEM((2, 2, 96, LANES), BF16),
            pltpu.VMEM((2, 2, 2, 96, LANES), BF16),
            pltpu.VMEM((2, 2, 2, 96, LANES), BF16),
            pltpu.VMEM((2, 2, 2, 96, LANES), BF16),
            pltpu.VMEM((2, 2, 2, 96, LANES), BF16),
            pltpu.VMEM((4, 384, LANES), F32),
            dma((15,)),
            dma((12,)),
            dma((12,)),
            dma((4,)),
            dma((4,)),
        ],
        compiler_params=pltpu.CompilerParams(
            collective_id=0, has_side_effects=True, vmem_limit_bytes=48 * 1024 * 1024
        ),
        name="residual_block",
    )(
        *(
            pltpu.with_memory_space_constraint(operand, pltpu.HBM)
            for operand in (
                latent.reshape(4, 768, LANES),
                clips,
                gain_in.reshape(1, 192),
                conv_in,
                bias_in.reshape(1, 96),
                gain_mid.reshape(1, 96),
                conv_mid,
                bias_mid.reshape(1, 96),
                skip_weight,
                skip_bias.reshape(1, 96),
            )
        )
    )
    return out.reshape(4, 96, 4, LANES)


def solution(mesh):
    n_t, n_r = mesh.shape["tm"], mesh.shape["rows"]
    return jax.shard_map(
        lambda *args: block(n_t, n_r, *args),
        mesh=mesh,
        in_specs=(P("tm", None, "rows", None),) + (P(),) * 9,
        out_specs=P("tm", None, "rows", None),
        check_vma=False,
    )
```

```python
import jax
import jax.numpy as jnp
from jax import lax
from jax.experimental import pallas as pl
from jax.experimental.pallas import tpu as pltpu
from jax.sharding import PartitionSpec as P

MESH = pl.DeviceIdType.MESH
F32 = jnp.float32
BF16 = jnp.bfloat16
EPS = 1e-6
LANES = 128
PARTS = ((1, 2), (0, 3))


def column(row_ref, scale=1.0):
    size = row_ref.shape[1]
    down = lax.broadcasted_iota(jnp.int32, (size, size), 0)
    across = lax.broadcasted_iota(jnp.int32, (size, size), 1)
    picked = jnp.where(down == across, row_ref[...] * scale, 0.0)
    return jnp.broadcast_to(jnp.sum(picked, axis=1, keepdims=True), (size, LANES))


def norm_silu(values, half_gain):
    mean_sq = jnp.mean(values * values, axis=0, keepdims=True)
    half = values * lax.rsqrt(mean_sq + EPS) * half_gain
    return half + half * jnp.tanh(half)


def put_shifts(x_ref, frame, row, values):
    lane = lax.broadcasted_iota(jnp.int32, values.shape, 1)
    left = jnp.where(lane == 0, 0.0, pltpu.roll(values, 1, 1))
    right = jnp.where(lane == LANES - 1, 0.0, pltpu.roll(values, LANES - 1, 1))
    x_ref[frame, row, 0] = left.astype(BF16)
    x_ref[frame, row, 2] = right.astype(BF16)


class Exchange:
    def __init__(self, copy, sends, gets):
        self.copy, self.sends, self.gets = copy, sends, gets


def body(
    n_t,
    n_r,
    latent_hbm,
    clips_hbm,
    gain_in_hbm,
    conv_in_hbm,
    bias_in_hbm,
    gain_mid_hbm,
    conv_mid_hbm,
    bias_mid_hbm,
    skip_hbm,
    skip_bias_hbm,
    out_ref,
    clips,
    gain_in,
    bias_in,
    gain_mid,
    bias_mid,
    skip_bias,
    latent_v,
    wide,
    raw,
    x1,
    x2,
    taps1,
    taps2,
    w1,
    w1_low,
    w2,
    w2_low,
    w_skip,
    col_in,
    col_bias,
    col_mid,
    col_out,
    acc1,
    acc2,
    edge_out,
    edge_in,
    corner_out1,
    corner_in1,
    corner_out2,
    corner_in2,
    sent1,
    got1,
    sent2,
    got2,
    packed,
    load_sem,
    row_send,
    row_recv,
    time_send,
    time_recv,
):
    t_at = lax.axis_index("tm")
    r_at = lax.axis_index("rows")
    has_up, has_down = r_at > 0, r_at < n_r - 1
    up, down = {"rows": r_at - 1}, {"rows": r_at + 1}
    has_before, has_after = t_at > 0, t_at < n_t - 1
    before, after = {"tm": t_at - 1}, {"tm": t_at + 1}

    barrier = pltpu.get_barrier_semaphore()
    def greet(*peers):
        for peer in peers:
            pl.semaphore_signal(barrier, inc=1, device_id=peer, device_id_type=MESH)

    pl.when(has_before)(lambda: greet(before))
    pl.when(has_up)(lambda: greet(up))
    pl.when(has_down)(lambda: greet(down))
    pl.when(has_before & has_up)(lambda: greet(before | up))
    pl.when(has_before & has_down)(lambda: greet(before | down))

    def load(src, dst, slot):
        return pltpu.make_async_copy(src, dst, load_sem.at[slot])

    load_gain = load(gain_in_hbm, gain_in, 0)
    load_latent = {f: load(latent_hbm.at[f], latent_v.at[f], 1 + f) for f in (2, 3, 0, 1)}
    load_taps = {i: load(conv_in_hbm.at[:, i], taps1.at[:, i], 5 + i) for i in (0, 2, 1)}
    load_clips = load(clips_hbm, clips, 8)
    load_bias = load(bias_in_hbm, bias_in, 9)
    load_mid = [load(gain_mid_hbm, gain_mid, 10), load(bias_mid_hbm, bias_mid, 11), load(skip_bias_hbm, skip_bias, 12)]
    load_mid += [load(skip_hbm, w_skip, 13), load(conv_mid_hbm, taps2, 14)]
    first_loads = [load_gain, load_clips, load_latent[2], load_latent[3], load_taps[0], load_taps[2]]
    first_loads += [load_latent[0], load_latent[1]]
    late_loads = [load_taps[1], load_bias] + load_mid
    for copy in first_loads + late_loads:
        copy.start()

    def clear(ref, *at):
        part = ref.at[at] if at else ref
        part[...] = jnp.zeros(part.shape, BF16)

    @pl.when(jnp.logical_not(has_up))
    def _():
        clear(edge_in, 1)
        for f in range(4):
            clear(x2, f, 0)

    @pl.when(jnp.logical_not(has_down))
    def _():
        clear(edge_in, 0)
        for f in range(4):
            clear(x2, f, 5)

    @pl.when(jnp.logical_not(has_before))
    def _():
        clear(got1)
        clear(got2)

    @pl.when(jnp.logical_not(has_before & has_up))
    def _():
        clear(corner_in1, 1)
        clear(corner_in2, 1)

    @pl.when(jnp.logical_not(has_before & has_down))
    def _():
        clear(corner_in1, 0)
        clear(corner_in2, 0)

    def remote(src, dst, sems, slot, peer, sends, gets):
        copy = pltpu.make_async_remote_copy(
            src_ref=src,
            dst_ref=dst,
            send_sem=sems[0].at[slot],
            recv_sem=sems[1].at[slot],
            device_id=peer,
            device_id_type=MESH,
        )
        return Exchange(copy, sends, gets)

    row_sems, time_sems = (row_send, row_recv), (time_send, time_recv)
    sides = ((up, has_up, has_down), (down, has_down, has_up))

    def by_row(src_of, dst_of, slot):
        return [remote(src_of(k), dst_of(k), row_sems, slot + k, *side) for k, side in enumerate(sides)]

    def by_corner(src, dst, slot):
        return [
            remote(src.at[k], dst.at[k], row_sems, slot + k, after | peer, sends & has_after, gets & has_before)
            for k, (peer, sends, gets) in enumerate(sides)
        ]

    def by_time(src, dst, slot):
        return [
            [remote(src.at[part], dst.at[part], time_sems, slot + part, after, has_after, has_before)]
            for part in range(2)
        ]

    rows1 = {g: by_row(lambda k: edge_out.at[k, pl.ds(g, 2)], lambda k: edge_in.at[k, pl.ds(g, 2)], g) for g in (2, 0)}
    rows2 = {
        f: by_row(lambda k: x2.at[pl.ds(f, 2), (1, 4)[k], 1], lambda k: x2.at[pl.ds(f, 2), (5, 0)[k], 1], 4 + f)
        for f in (2, 0)
    }
    corners1 = by_corner(corner_out1, corner_in1, 8)
    corners2 = by_corner(corner_out2, corner_in2, 10)
    times1 = by_time(sent1, got1, 0)
    times2 = by_time(sent2, got2, 2)

    def start(*exchanges):
        for sides_of in zip(*exchanges):

            @pl.when(sides_of[0].sends)
            def _(sides_of=sides_of):
                for exchange in sides_of:
                    exchange.copy.start()

    def arrived(*exchanges):
        for sides_of in zip(*exchanges):

            @pl.when(sides_of[0].gets)
            def _(sides_of=sides_of):
                for exchange in sides_of:
                    exchange.copy.wait_recv()

    def left(*exchanges):
        for sides_of in zip(*exchanges):

            @pl.when(sides_of[0].sends)
            def _(sides_of=sides_of):
                for exchange in sides_of:
                    exchange.copy.wait_send()

    def spread(frame):
        wide[frame] = latent_v[frame].astype(F32)

    def first_act(frame, rows):
        for row in rows:
            values = wide[frame, pl.ds(row, 192, stride=4), :]
            raw[frame, row] = values.astype(BF16)
            act = norm_silu(values, col_in[...])
            x1[frame, row, 1] = act.astype(BF16)
            put_shifts(x1, frame, row, act)

    seen = set()

    def gather(acc, first, row, terms, taps, base, keeps_target):
        sums = {}
        for k, f in enumerate((first, first + 1)):
            for n, tap in enumerate(taps):
                target = f + 2 - tap
                if not keeps_target(target):
                    continue
                value = terms[n * 96 : (n + 1) * 96, k * LANES : (k + 1) * LANES]
                if target > f:
                    value = value * keeps[target, target - f]
                sums[target] = value if target not in sums else sums[target] + value
        for target, value in sums.items():
            key = (id(acc), target, row)
            if key in seen:
                value = value + acc[target, row]
            elif base is not None and target < 4 and 1 <= row <= 4:
                value = value + base
            seen.add(key)
            acc[target, row] = value

    sources = {-1: (0,), 0: (1, 0), 1: (0, 1, 2), 2: (1, 2, 3), 3: (2, 3), 4: (3,)}

    def conv1(first, targets):
        for target in targets:
            rows = sources[target]
            slab = jnp.concatenate(
                [jnp.concatenate([x1[f, row].reshape(576, LANES) for row in rows], axis=0) for f in (first, first + 1)],
                axis=1,
            )
            weight = (w1_low if target < 1 else w1)[:, : 576 * len(rows)]
            terms = jnp.dot(weight, slab, preferred_element_type=F32)
            gather(acc1, first, target + 1, terms, (0, 1, 2), col_bias[...] if 0 <= target < 4 else None, lambda g: True)

    def conv2_part(first, target, rows, weight, taps, keeps_target):
        slab = jnp.concatenate(
            [jnp.concatenate([x2[f, row + 1].reshape(288, LANES) for row in rows], axis=0) for f in (first, first + 1)],
            axis=1,
        )
        weight = weight[pl.ds(96 * taps[0], 96 * len(taps)), : 288 * len(rows)]
        terms = jnp.dot(weight, slab, preferred_element_type=F32)
        gather(acc2, first, target + 1, terms, taps, None, keeps_target)

    def conv2(first, targets):
        for target in targets:
            weight = w2_low if target < 1 else w2
            if target in (-1, 4):
                conv2_part(first, target, sources[target], weight, (0, 1), lambda g: g >= 4)
            else:
                conv2_part(first, target, sources[target], weight, (0, 1, 2), lambda g: True)

    def halo2(first):
        for row in (0, 5):
            for frame in (first, first + 1):
                put_shifts(x2, frame, row, x2[frame, row, 1].astype(F32))
        taps = (1, 2) if first == 2 else (0, 1, 2)
        conv2_part(first, 0, (-1,), w2, taps, lambda g: g < 4)
        conv2_part(first, 3, (4,), w2_low, taps, lambda g: g < 4)

    def edges_out(g):
        for k, row in enumerate((0, 5)):
            for frame in (g, g + 1):
                edge_out[k, frame] = acc1[frame, row].astype(BF16)

    def corners_out(acc, buf):
        for k, row in enumerate((0, 5)):
            for g in range(2):
                buf[k, g] = acc[4 + g, row].astype(BF16)

    def pass_on(acc, buf, copies, part):
        for g in range(2):
            for k, row in enumerate(PARTS[part]):
                buf[part, g, k] = acc[4 + g, row + 1].astype(BF16)
        start(copies[part])

    def with_time(values, frame, row, got, corner):
        if frame < 2:
            part = 1 if row in (0, 3) else 0
            values = values + got[part, frame, PARTS[part].index(row)].astype(F32)
            if part:
                values = values + corner[1 if row == 0 else 0, frame].astype(F32)
        return values

    def second_act(frame, part, shifted=True):
        for row in PARTS[part]:
            values = acc1[frame, row + 1]
            if part:
                values = values + edge_in[1 if row == 0 else 0, frame].astype(F32)
            values = with_time(values, frame, row, got1, corner_in1)
            act = norm_silu(values, col_mid[...])
            x2[frame, row + 1, 1] = act.astype(BF16)
            if shifted:
                put_shifts(x2, frame, row + 1, act)

    def shift_edges(first):
        for frame in (first, first + 1):
            for row in (1, 4):
                put_shifts(x2, frame, row, x2[frame, row, 1].astype(F32))

    def shortcut(row):
        slab = jnp.concatenate([raw[f, row] for f in range(4)], axis=1)
        terms = jnp.dot(w_skip[...], slab, preferred_element_type=F32)
        for f in range(4):
            acc2[f, row + 1] = terms[:, f * LANES : (f + 1) * LANES] + col_out[...]
            seen.add((id(acc2), f, row + 1))

    def finish(frame, part):
        for row in PARTS[part]:
            packed[frame, pl.ds(row, 96, stride=4), :] = with_time(acc2[frame, row + 1], frame, row, got2, corner_in2)

    def pack(dst, src, block, row_tap, size):
        for tap in range(3):
            dst[pl.ds(tap * 96, 96), pl.ds(block * 3 * size, 3 * size)] = jnp.concatenate(
                [src[tap, row_tap, k] for k in range(3)], axis=1
            )

    load_gain.wait()
    col_in[...] = column(gain_in, 0.5)
    load_clips.wait()
    total = clips.shape[0]

    def keep(frame, back):
        at = t_at * 4 + frame
        own = clips[jnp.minimum(at, total - 1)]
        past = clips[jnp.clip(at - back, 0, total - 1)]
        good = (own == past) & (at < total) & (at >= back)
        return jnp.where(good, 1.0, 0.0).astype(F32)

    keeps = {(f, d): keep(f, d) for f in range(1, 6) for d in (1, 2) if 0 <= f - d < 4}
    for copy in first_loads[2:]:
        copy.wait()
    pack(w1, taps1, 0, 0, 192)
    pack(w1_low, taps1, 0, 2, 192)
    for frame in (2, 3, 0, 1):
        spread(frame)
        first_act(frame, (0, 3))
    conv1(2, (-1, 4))
    conv1(0, (-1, 4))
    edges_out(2)
    edges_out(0)
    corners_out(acc1, corner_out1)
    friends = (has_up, has_down, has_after, has_after & has_up, has_after & has_down)
    greeted = sum(there.astype(jnp.int32) for there in friends)
    pl.semaphore_wait(barrier, greeted)
    start(rows1[2])
    start(corners1)
    start(rows1[0])
    load_taps[1].wait()
    load_bias.wait()
    col_bias[...] = column(bias_in)
    for tap in range(3):
        at = pl.ds(tap * 96, 96)
        middle = [taps1[tap, 1, k] for k in range(3)]
        last = [taps1[tap, 2, k] for k in range(3)]
        w1[at, pl.ds(512, 1216)] = jnp.concatenate([w1[at, pl.ds(512, 64)]] + middle + last, axis=1)
        w1_low[at, pl.ds(512, 640)] = jnp.concatenate([w1_low[at, pl.ds(512, 64)]] + middle, axis=1)
    for frame in (2, 3):
        first_act(frame, (1, 2))
    conv1(2, (0, 3))
    pass_on(acc1, sent1, times1, 1)
    conv1(2, (1, 2))
    pass_on(acc1, sent1, times1, 0)
    for frame in (0, 1):
        first_act(frame, (1, 2))
    conv1(0, (0, 3, 1, 2))
    for copy in load_mid:
        copy.wait()
    col_mid[...] = column(gain_mid, 0.5)
    col_out[...] = column(bias_mid) + column(skip_bias)
    for tap in range(3):
        rest = [taps2[tap, i, k] for i in (0, 1, 2) for k in range(3)]
        w2[pl.ds(tap * 96, 96), :] = jnp.concatenate(rest, axis=1)
        w2_low[pl.ds(tap * 96, 96), :] = jnp.concatenate(rest[6:] + rest[3:6], axis=1)
    for frame in (2, 3):
        second_act(frame, 0)
    for row in range(4):
        shortcut(row)
    arrived(rows1[2])
    for frame in (2, 3):
        second_act(frame, 1, shifted=False)
    start(rows2[2])
    shift_edges(2)
    conv2(2, (0, 3))
    pass_on(acc2, sent2, times2, 1)
    conv2(2, (-1, 4))
    corners_out(acc2, corner_out2)
    start(corners2)
    arrived(rows1[0])
    arrived(corners1)
    arrived(times1[1])
    for frame in (0, 1):
        second_act(frame, 1, shifted=False)
    start(rows2[0])
    shift_edges(0)
    conv2(2, (1, 2))
    pass_on(acc2, sent2, times2, 0)
    arrived(times1[0])
    for frame in (0, 1):
        second_act(frame, 0)
    conv2(0, (0, 3, 1, 2))
    arrived(rows2[2])
    halo2(2)
    for frame in (2, 3):
        finish(frame, 0)
    arrived(times2[0], times2[1])
    arrived(corners2)
    arrived(rows2[0])
    for frame in (0, 1):
        finish(frame, 0)
    halo2(0)
    for frame in range(4):
        finish(frame, 1)
        out_ref[frame] = packed[frame].astype(BF16)
    left(rows1[2], rows1[0], rows2[2], rows2[0])
    left(corners1, corners2)
    left(*times1, *times2)


def block(n_t, n_r, latent, clips, gain_in, conv_in, bias_in, gain_mid, conv_mid, bias_mid, skip_weight, skip_bias):
    hbm = pl.BlockSpec(memory_space=pltpu.HBM)
    dma = pltpu.SemaphoreType.DMA
    out = pl.pallas_call(
        lambda *refs: body(n_t, n_r, *refs),
        out_shape=pltpu.VMEM((4, 384, LANES), BF16),
        in_specs=[hbm] * 10,
        out_specs=pl.BlockSpec(memory_space=pltpu.VMEM),
        scratch_shapes=[
            pltpu.SMEM(clips.shape, jnp.int32),
            pltpu.VMEM((1, 192), F32),
            pltpu.VMEM((1, 96), F32),
            pltpu.VMEM((1, 96), F32),
            pltpu.VMEM((1, 96), F32),
            pltpu.VMEM((1, 96), F32),
            pltpu.VMEM((4, 768, LANES), BF16),
            pltpu.VMEM((4, 768, LANES), F32),
            pltpu.VMEM((4, 4, 192, LANES), BF16),
            pltpu.VMEM((4, 4, 3, 192, LANES), BF16),
            pltpu.VMEM((4, 6, 3, 96, LANES), BF16),
            pltpu.VMEM((3, 3, 3, 96, 192), BF16),
            pltpu.VMEM((3, 3, 3, 96, 96), BF16),
            pltpu.VMEM((288, 1728), BF16),
            pltpu.VMEM((288, 1152), BF16),
            pltpu.VMEM((288, 864), BF16),
            pltpu.VMEM((288, 576), BF16),
            pltpu.VMEM((96, 192), BF16),
            pltpu.VMEM((192, LANES), F32),
            pltpu.VMEM((96, LANES), F32),
            pltpu.VMEM((96, LANES), F32),
            pltpu.VMEM((96, LANES), F32),
            pltpu.VMEM((6, 6, 96, LANES), F32),
            pltpu.VMEM((6, 6, 96, LANES), F32),
            pltpu.VMEM((2, 4, 96, LANES), BF16),
            pltpu.VMEM((2, 4, 96, LANES), BF16),
            pltpu.VMEM((2, 2, 96, LANES), BF16),
            pltpu.VMEM((2, 2, 96, LANES), BF16),
            pltpu.VMEM((2, 2, 96, LANES), BF16),
            pltpu.VMEM((2, 2, 96, LANES), BF16),
            pltpu.VMEM((2, 2, 2, 96, LANES), BF16),
            pltpu.VMEM((2, 2, 2, 96, LANES), BF16),
            pltpu.VMEM((2, 2, 2, 96, LANES), BF16),
            pltpu.VMEM((2, 2, 2, 96, LANES), BF16),
            pltpu.VMEM((4, 384, LANES), F32),
            dma((15,)),
            dma((12,)),
            dma((12,)),
            dma((4,)),
            dma((4,)),
        ],
        compiler_params=pltpu.CompilerParams(
            collective_id=0, has_side_effects=True, vmem_limit_bytes=48 * 1024 * 1024
        ),
        name="residual_block",
    )(
        *(
            pltpu.with_memory_space_constraint(operand, pltpu.HBM)
            for operand in (
                latent.reshape(4, 768, LANES),
                clips,
                gain_in.reshape(1, 192),
                conv_in,
                bias_in.reshape(1, 96),
                gain_mid.reshape(1, 96),
                conv_mid,
                bias_mid.reshape(1, 96),
                skip_weight,
                skip_bias.reshape(1, 96),
            )
        )
    )
    return out.reshape(4, 96, 4, LANES)


def solution(mesh):
    n_t, n_r = mesh.shape["tm"], mesh.shape["rows"]
    return jax.shard_map(
        lambda *args: block(n_t, n_r, *args),
        mesh=mesh,
        in_specs=(P("tm", None, "rows", None),) + (P(),) * 9,
        out_specs=P("tm", None, "rows", None),
        check_vma=False,
    )
```
